32 devices in a mesh: slab: 2 (over y), ty: 4 (over x, core), tx: 4 (over z).
Axes of the slice: x: 2, y: 2, z: 4, core: 2. Of those that a mesh axis runs over, the one named last changes fastest.
Arguments:
- mask_logits: float32 [1024, 512], P(('slab', 'ty'), 'tx'), parts along dimension 0, may hold values from -8 to 8
- target: int32 [1024, 512], P(('slab', 'ty'), 'tx'), parts along dimension 0, may hold values 0 or 1
- weight: float32 [1024, 512], P(('slab', 'ty'), 'tx'), parts along dimension 0, may hold values from 0.5 to 162
- spectra: float32 [7, 2, 256, 256], replicated, may hold values from -6 to 6, as said below
Outputs:
- new_logits: float32 [1024, 512], P(('slab', 'ty'), 'tx'), parts along dimension 0
- resist: float32 [1024, 512], P(('slab', 'ty'), 'tx'), parts along dimension 0
- losses: float32 [4], P('slab'), parts along dimension 0
The draws below stay inside these ranges and needn't reach their ends.
There are 2 independent parts, one for each index of `slab`. The reference program is written for one: setup_inputs(seed, part) draws one part's arguments, and reference() takes and returns one part's arrays. A program takes and returns all parts, laid end to end along the dimension named above; an argument that names none is the same for every part. Nothing has to cross between parts.
Inputs may be any that keep to these rules, and one draw needn't show every extreme that they name: `spectra`: each kernel k is the transform over the 256 x 256 grid of taps that lie only at offsets -64 to 63 along each dimension.
All inputs are finite; a program needn't handle non-finite values. No bound on the sum of `target` on one device may be relied on, other than what follows from the above.
Results may differ from the reference program's by a relative error of at most 0.00013.
Values sent between devices are 32-bit elements; how exact they have to be, the bound alone decides.
A program may use at most 64 MiB of HBM per device.

```python
import math
import jax
import jax.numpy as jnp
from jax import lax

H = 64
KERN = 7
ITERS = 2
E = 256
NY = 512
NX = 512


def draw_weight(key, part):
    base = jax.random.fold_in(key, 11)
    rows = jnp.arange(NY, dtype=jnp.int32).astype(jnp.float32) / NY
    cols = jnp.arange(NX, dtype=jnp.int32).astype(jnp.float32) / NX
    ramp = jnp.exp(math.log(4.0) * (rows[:, None] + cols[None, :]))
    rough = jnp.exp(jax.random.uniform(base, (NY, NX), jnp.float32, math.log(0.5), math.log(2.0)))
    return ramp * rough


def draw_spectra(key, part):
    base = jax.random.fold_in(key, 23)
    spread = 1.0 / math.sqrt(KERN * 2.0 * (2 * H) * (2 * H) * 0.4)
    taps = jax.random.normal(base, (KERN, 2, 2 * H, 2 * H), jnp.float32) * spread
    freqs = jnp.arange(E, dtype=jnp.int32)
    offsets = jnp.arange(2 * H, dtype=jnp.int32) - H
    phase = freqs[:, None] * offsets[None, :] % E
    angle = phase.astype(jnp.float32) * (2.0 * math.pi / E)
    table_re = jnp.cos(angle)
    table_im = -jnp.sin(angle)
    fine = lax.Precision.HIGHEST
    taps_re = taps[:, 0]
    taps_im = taps[:, 1]
    first_re = jnp.einsum('fa,kab->kfb', table_re, taps_re, precision=fine) - jnp.einsum('fa,kab->kfb', table_im, taps_im, precision=fine)
    first_im = jnp.einsum('fa,kab->kfb', table_re, taps_im, precision=fine) + jnp.einsum('fa,kab->kfb', table_im, taps_re, precision=fine)
    spec_re = jnp.einsum('kfb,gb->kfg', first_re, table_re, precision=fine) - jnp.einsum('kfb,gb->kfg', first_im, table_im, precision=fine)
    spec_im = jnp.einsum('kfb,gb->kfg', first_re, table_im, precision=fine) + jnp.einsum('kfb,gb->kfg', first_im, table_re, precision=fine)
    return jnp.stack([spec_re, spec_im], axis=1)


def set_ends(values, own_key, low, top_value):
    place = [jax.random.randint(jax.random.fold_in(own_key, axis), (), 0, length) for axis, length in enumerate(values.shape)]
    main_axis = values.shape.index(max(values.shape))
    neighbour = place[:main_axis] + [(place[main_axis] + 1) % values.shape[main_axis]] + place[main_axis + 1:]
    return values.at[tuple(place)].set(low).at[tuple(neighbour)].set(top_value)


def block_levels(key, shape, pieces, smallest, high):
    gain = 1.0
    for dim, blocks in pieces:
        steps = jax.random.uniform(jax.random.fold_in(jax.random.fold_in(key, 6), dim), (blocks,), jnp.float32, smallest / len(pieces), high / len(pieces))
        gain = gain * jnp.repeat(jnp.exp(steps), shape[dim] // blocks).reshape((-1,) + (1,) * (len(shape) - 1 - dim))
    return gain


def noise(rng, extent, deviation, limit, cuts=(), kind=jnp.bfloat16):
    result = deviation * jax.random.normal(rng, extent, jnp.float32)
    if cuts:
        result = result * block_levels(rng, extent, cuts, -0.22, 0.18)
    return jnp.clip(result, -limit, limit).astype(kind)


def setup_inputs(seed: int = 0, part: int = 0) -> dict:
    splits = jax.random.split(jax.random.key(seed), 5)
    part_keys = jax.random.split(jax.random.fold_in(splits[4], part), 5)
    mask_logits = noise(part_keys[0], (NY, NX), 2.0, 8.0, ((0, 4), (1, 4)), jnp.float32)
    target = set_ends((jax.random.randint(part_keys[1], (NY, NX), 0, 2) < 1).astype(jnp.int32), jax.random.fold_in(part_keys[1], 1), 0, 1)
    weight = draw_weight(jax.random.fold_in(jax.random.fold_in(splits[4], part), 71), part)
    spectra = draw_spectra(jax.random.fold_in(splits[4], 71), part)
    return {"mask_logits": mask_logits, "target": target, "weight": weight, "spectra": spectra}


def reference(mask_logits, target, weight, spectra):
    kern_c = spectra[:, 0] + 1j * spectra[:, 1]
    taps = jnp.fft.ifft2(kern_c, axes=(1, 2))
    taps = jnp.roll(taps, (H, H), axis=(1, 2))[:, :2 * H, :2 * H]
    rows_all = mask_logits.shape[0]
    cols_all = mask_logits.shape[1]
    pad_rows = rows_all + 2 * H
    pad_cols = cols_all + 2 * H
    placed = jnp.pad(taps, ((0, 0), (0, pad_rows - 2 * H), (0, pad_cols - 2 * H)))
    placed = jnp.roll(placed, (-H, -H), axis=(1, 2))
    kern_f = jnp.fft.fft2(placed, axes=(1, 2))
    truth = target.astype(jnp.float32)
    pixels = rows_all * cols_all

    def objective(logits):
        layout = jax.nn.sigmoid(logits)
        layout_f = jnp.fft.fft2(jnp.pad(layout, ((0, 2 * H), (0, 2 * H))))
        image = jnp.zeros((rows_all, cols_all), jnp.float32)
        for kernel in range(KERN):
            field = jnp.fft.ifft2(layout_f * kern_f[kernel])[:rows_all, :cols_all]
            image = image + jnp.real(field) * jnp.real(field) + jnp.imag(field) * jnp.imag(field)
        resist = jax.nn.sigmoid(4.0 * (image - 1.0))
        miss = resist - truth
        return (jnp.sum(weight * miss * miss), resist)
    params = mask_logits
    loss_list = []
    resist = None
    for iteration in range(ITERS):
        (value, resist), grad = jax.value_and_grad(objective, has_aux=True)(params)
        loss_list.append(value / pixels)
        norm = jnp.sqrt(jnp.sum(grad * grad) / pixels + 1e-06)
        params = params - grad / norm
    return (params, resist, jnp.stack(loss_list))
```

```python
import functools
import math

import jax
import jax.numpy as jnp
import numpy as np
from jax import lax
from jax.experimental import pallas as pl
from jax.experimental.pallas import tpu as pltpu
from jax.sharding import PartitionSpec as P

ITERS = 2
STEEPNESS = 4.0
THRESHOLD = 1.0
EPSILON = 1e-06
F32 = jnp.float32
BF16 = jnp.bfloat16
MESH = pl.DeviceIdType.MESH
DIRS = ((-1, 0), (1, 0), (0, -1), (0, 1), (-1, -1), (-1, 1), (1, -1), (1, 1))
OPPOSITE = tuple(DIRS.index((-dy, -dx)) for dy, dx in DIRS)


def split(x):
    high = x.astype(BF16)
    return high, (x - high.astype(F32)).astype(BF16)


def dot(a, b):
    return lax.dot_general(a, b, (((1,), (0,)), ((), ())), preferred_element_type=F32)


def dot3(left, right):
    lh, ll = left
    rh, rl = right
    return dot(lh, rh) + (dot(ll, rh) + dot(lh, rl))


def sigmoid(x):
    return 1.0 / (1.0 + jnp.exp(-x))


def kernel(
    ny, nx,
    logits_ref, target_ref, weight_ref, spectra_hbm, table_ref,
    params_out, resist_out, loss_out,
    spec, t2, t3, t4, t5, t6, t7, pw, fields, total,
    send_edge, send_corner, recv_edge, recv_corner, sums_send, sums_recv,
    spec_sem, send_sem, recv_sem, sums_send_sem, sums_recv_sem,
):
    side = logits_ref.shape[0]
    extent = spec.shape[2]
    kern = spec.shape[0]
    rim = (extent - side) // 2
    ty, tx = lax.axis_index("ty"), lax.axis_index("tx")
    count = ny * nx
    me = ty * nx + tx
    pixels = float(side * side * count)

    spec_copy = pltpu.make_async_copy(spectra_hbm, spec, spec_sem)
    spec_copy.start()

    barrier = pltpu.get_barrier_semaphore()

    def peer_id(step):
        peer = lax.rem(me + step, count)
        return {"ty": peer // nx, "tx": lax.rem(peer, nx)}

    def greet(step, carry):
        pl.semaphore_signal(barrier, inc=1, device_id=peer_id(step), device_id_type=MESH)
        return carry

    lax.fori_loop(1, count, greet, 0)

    def exists(d):
        dy, dx = DIRS[d]
        ok = None
        for at, step, size in ((ty, dy, ny), (tx, dx, nx)):
            if step:
                here = at > 0 if step < 0 else at < size - 1
                ok = here if ok is None else jnp.logical_and(ok, here)
        return ok

    def buffers(d):
        return (send_edge, recv_edge, d) if d < 4 else (send_corner, recv_corner, d - 4)

    def start(phase, pieces):
        for d, piece in enumerate(pieces):
            buf, _, slot = buffers(d)
            buf[phase, slot] = piece
        for d, (dy, dx) in enumerate(DIRS):
            src, dst, slot = buffers(d)
            _, _, there = buffers(OPPOSITE[d])

            @pl.when(exists(d))
            def _():
                pltpu.make_async_remote_copy(
                    src_ref=src.at[phase, slot],
                    dst_ref=dst.at[phase, there],
                    send_sem=send_sem.at[phase, d],
                    recv_sem=recv_sem.at[phase, OPPOSITE[d]],
                    device_id={"ty": ty + dy, "tx": tx + dx},
                    device_id_type=MESH,
                ).start()

    def finish(phase):
        for d, (dy, dx) in enumerate(DIRS):
            src, dst, slot = buffers(d)

            @pl.when(exists(d))
            def _():
                pltpu.make_async_remote_copy(
                    src_ref=src.at[phase, slot],
                    dst_ref=dst.at[phase, slot],
                    send_sem=send_sem.at[phase, d],
                    recv_sem=recv_sem.at[phase, d],
                    device_id={"ty": ty + dy, "tx": tx + dx},
                    device_id_type=MESH,
                ).wait()

    def lanes(rows):
        return lax.broadcasted_iota(jnp.int32, (rows, side), 1)

    def pack(x, low):
        half = x.shape[0] // 2
        a, b = x[:half], pltpu.roll(x[half:], rim, 1)
        first = lanes(half) < rim
        return jnp.where(first, a, b) if low else jnp.where(first, b, a)

    def unpack(p):
        return jnp.concatenate([p, pltpu.roll(p, rim, 1)], axis=0)

    def rows_of(x, dy, low):
        if dy == 0:
            return x
        return x[:rim] if low else x[rim:]

    def halo_pieces(own):
        out = []
        for dy, dx in DIRS:
            piece = rows_of(own, dy, dy < 0)
            out.append(pack(piece, dx < 0) if dx else piece)
        return out

    def got(phase, dy, dx):
        _, buf, slot = buffers(DIRS.index((dy, dx)))
        value = buf[phase, slot]
        return unpack(value) if dx else value

    def halo_quads(phase, own):
        def beside(dy):
            right, left = got(phase, dy, 1), got(phase, dy, -1)
            return jnp.where(lanes(right.shape[0]) < rim, right, left)

        below = jnp.concatenate([got(phase, 1, 0), got(phase, -1, 0)], axis=0)
        corner = jnp.concatenate([beside(1), beside(-1)], axis=0)
        return ((own, beside(0)), (below, corner))

    def edge_mask(at, size, dim):
        where = lax.broadcasted_iota(jnp.int32, (side, side), dim)
        after = jnp.where(at < size - 1, rim, 0)
        before = jnp.where(at > 0, rim, side)
        return jnp.logical_or(where < after, where >= before)

    col_ok = edge_mask(tx, nx, 1)
    row_ok = edge_mask(ty, ny, 0)

    def masked(quads):
        (a, b), (c, d) = quads
        b = jnp.where(col_ok, b, 0.0)
        c = jnp.where(row_ok, c, 0.0)
        d = jnp.where(jnp.logical_and(row_ok, col_ok), d, 0.0)
        return jnp.concatenate(
            [jnp.concatenate([a, b], axis=1), jnp.concatenate([c, d], axis=1)], axis=0
        )

    def each(f, *quads):
        return tuple(tuple(f(*(q[i][j] for q in quads)) for j in range(2)) for i in range(2))

    def fold_pieces(partial):
        out = []
        for dy, dx in DIRS:
            piece = partial[side:] if dy else partial[:side]
            piece = piece[:, side:] if dx else piece[:, :side]
            piece = rows_of(piece, dy, dy > 0)
            out.append(pack(piece, dx > 0) if dx else piece)
        return out

    def fold(phase, own):
        zero = jnp.zeros((rim, side), F32)
        for d, (dy, dx) in enumerate(DIRS):
            value = got(phase, dy, dx)
            here = jnp.where(exists(d), 1, 0)
            if dx:
                lane = lanes(value.shape[0])
                near = jnp.where(lane >= rim, 1, 0) if dx > 0 else jnp.where(lane < rim, 1, 0)
                keep = near * here > 0
            else:
                keep = jnp.full(value.shape, here, jnp.int32) > 0
            value = jnp.where(keep, value, 0.0)
            if dy:
                value = jnp.concatenate([zero, value] if dy > 0 else [value, zero], axis=0)
            own = own + value
        return own

    def total_start(phase, row):
        sums_send[phase] = row
        sums_recv[phase, me] = row

        def send(step, carry):
            pltpu.make_async_remote_copy(
                src_ref=sums_send.at[phase],
                dst_ref=sums_recv.at[phase, me],
                send_sem=sums_send_sem.at[phase],
                recv_sem=sums_recv_sem.at[phase],
                device_id=peer_id(step),
                device_id_type=MESH,
            ).start()
            return carry

        lax.fori_loop(1, count, send, 0)

    def total_finish(phase):
        if count > 1:
            every = sums_recv.at[phase, pl.ds(0, count - 1)]
            pltpu.make_async_copy(every, every, sums_recv_sem.at[phase]).wait()
            pltpu.make_async_copy(every, every, sums_send_sem.at[phase]).wait()
        return jnp.sum(sums_recv[phase], axis=0)

    for part in range(2):
        cos, sin = table_ref[part, :, :extent], table_ref[part, :, extent:]
        t2[part, :extent], t2[part, extent:] = cos, sin
        cd, sd = cos[:, :side], sin[:, :side]
        unit = jnp.asarray(1.0 / (extent * extent), BF16)
        t3[part, :extent, :side], t3[part, :extent, side:] = cd * unit, sd * unit
        t3[part, extent:, :side], t3[part, extent:, side:] = -sd * unit, cd * unit
        cc, sc = cos[:side], sin[:side]
        t4[part, :side], t4[part, side:] = cc, sc
        t5[part, :side, :extent], t5[part, :side, extent:] = cc, sc
        t5[part, side:, :extent], t5[part, side:, extent:] = sc, -cc
        t6[part, :extent, :side], t6[part, :extent, side:] = cd, -sd
        t6[part, extent:, :side], t6[part, extent:, side:] = sd, cd
        t7[part, :extent, :extent], t7[part, :extent, extent:] = cos, -sin
        t7[part, extent:, :extent], t7[part, extent:, extent:] = sin, cos

    def both(ref):
        return ref[0], ref[1]

    truth = target_ref[...].astype(F32)
    weight = weight_ref[...]
    params = logits_ref[...]

    pl.semaphore_wait(barrier, count - 1)
    start(0, halo_pieces(params))
    loss_rows = []
    grad = norm = None
    for iteration in range(ITERS):
        halo_phase, fold_phase = 2 * iteration, 2 * iteration + 1
        finish(halo_phase)
        if iteration == 0:
            quads = halo_quads(halo_phase, params)
        else:
            old = each(lambda x: x, tuple(
                tuple(pw[i * side:(i + 1) * side, j * side:(j + 1) * side] for j in range(2))
                for i in range(2)))
            quads = each(lambda p, g: p - g / norm, old, halo_quads(halo_phase, grad))
        params = quads[0][0]
        if iteration + 1 < ITERS:
            for i in range(2):
                for j in range(2):
                    pw[i * side:(i + 1) * side, j * side:(j + 1) * side] = quads[i][j]
        wide = masked(each(sigmoid, quads))
        layout = wide[:side, :side]
        mixed = dot3(split(wide), both(table_ref))
        four = dot3(both(t2), split(mixed))
        trans_re = four[:extent, :extent] - four[extent:, extent:]
        trans_im = -(four[:extent, extent:] + four[extent:, :extent])
        total[0], total[1] = trans_re, trans_im
        if iteration == 0:
            spec_copy.wait()

        def forward(k, image):
            sr, si = spec[k, 0], spec[k, 1]
            tr, ti = total[0], total[1]
            prod = jnp.concatenate([tr * sr - ti * si, tr * si + ti * sr], axis=1)
            half = dot3(split(prod), both(t3))
            quad = dot3(both(t4), split(half))
            re = quad[:side, :side] - quad[side:, side:]
            im = quad[:side, side:] + quad[side:, :side]
            fields[k, :, :side] = re
            fields[k, :, side:] = im
            return image + (re * re + im * im)

        image = lax.fori_loop(0, kern, forward, jnp.zeros((side, side), F32))
        resist = sigmoid(STEEPNESS * (image - THRESHOLD))
        missed = resist - truth
        loss_rows.append(jnp.sum(weight * missed * missed, axis=0, keepdims=True))
        g_image = (2.0 * STEEPNESS) * weight * missed * resist * (1.0 - resist)
        g_image = g_image * (2.0 / (extent * extent))
        g_twice = jnp.concatenate([g_image, g_image], axis=1)
        total[...] = jnp.zeros_like(total)

        def backward(k, carry):
            back = fields[k] * g_twice
            x = dot3(split(back), both(t5))
            x = jnp.concatenate([x[:, :extent], x[:, extent:]], axis=0)
            full = dot3(both(t6), split(x))
            fr, fi = full[:extent], full[extent:]
            sr, si = spec[k, 0], spec[k, 1]
            total[0] += fr * sr - fi * si
            total[1] += fr * si + fi * sr
            return carry

        lax.fori_loop(0, kern, backward, 0)
        sums = jnp.concatenate([total[0], total[1]], axis=1)
        y = dot3(split(sums), both(t7))
        y = jnp.concatenate([y[:, :extent], y[:, extent:]], axis=0)
        partial = dot3(both(table_ref), split(y))
        start(fold_phase, fold_pieces(partial))
        finish(fold_phase)
        g_layout = fold(fold_phase, partial[:side, :side])
        grad = g_layout * layout * (1.0 - layout)
        square = jnp.sum(grad * grad, axis=0, keepdims=True)
        last = iteration + 1 == ITERS
        rows = loss_rows if last else [square] * ITERS
        total_start(iteration, jnp.concatenate([square] + rows, axis=1))
        if not last:
            start(halo_phase + 2, halo_pieces(grad))
        else:
            resist_out[...] = resist
        everyone = total_finish(iteration)
        sq_all = jnp.sum(everyone[:, :side], axis=1, keepdims=True)
        norm = jnp.sqrt(sq_all / pixels + EPSILON)
    params_out[...] = params - grad / norm
    for i in range(ITERS):
        row = everyone[:, (i + 1) * side:(i + 2) * side]
        value = jnp.sum(row, axis=1, keepdims=True) / pixels
        loss_out[i:i + 1, :] = jnp.broadcast_to(value, (1, side))


def tables(extent):
    index = np.arange(extent)
    angle = (index[:, None] * index[None, :] % extent) * (2.0 * math.pi / extent)
    exact = np.concatenate([np.cos(angle), np.sin(angle)], axis=1)
    high = exact.astype(jnp.bfloat16)
    low = (exact - high.astype(np.float64)).astype(jnp.bfloat16)
    return np.stack([high, low])


def on_device(ny, nx, logits, target, weight, spectra):
    side = logits.shape[0]
    kern, _, extent, _ = spectra.shape
    rim = (extent - side) // 2
    count = ny * nx
    phases = 2 * ITERS
    vmem = pl.BlockSpec(memory_space=pltpu.VMEM)
    params, resist, losses = pl.pallas_call(
        functools.partial(kernel, ny, nx),
        out_shape=(
            jax.ShapeDtypeStruct((side, side), F32),
            jax.ShapeDtypeStruct((side, side), F32),
            jax.ShapeDtypeStruct((8, side), F32),
        ),
        in_specs=[vmem, vmem, vmem, pl.BlockSpec(memory_space=pl.ANY), vmem],
        out_specs=(vmem, vmem, vmem),
        scratch_shapes=[
            pltpu.VMEM(spectra.shape, F32),
            pltpu.VMEM((2, 2 * extent, extent), BF16),
            pltpu.VMEM((2, 2 * extent, 2 * side), BF16),
            pltpu.VMEM((2, 2 * side, extent), BF16),
            pltpu.VMEM((2, 2 * side, 2 * extent), BF16),
            pltpu.VMEM((2, 2 * extent, 2 * side), BF16),
            pltpu.VMEM((2, 2 * extent, 2 * extent), BF16),
            pltpu.VMEM((extent, extent), F32),
            pltpu.VMEM((kern, side, 2 * side), F32),
            pltpu.VMEM((2, extent, extent), F32),
            pltpu.VMEM((phases, 4, rim, side), F32),
            pltpu.VMEM((phases, 4, rim // 2, side), F32),
            pltpu.VMEM((phases, 4, rim, side), F32),
            pltpu.VMEM((phases, 4, rim // 2, side), F32),
            pltpu.VMEM((ITERS, 1, (1 + ITERS) * side), F32),
            pltpu.VMEM((ITERS, count, 1, (1 + ITERS) * side), F32),
            pltpu.SemaphoreType.DMA,
            pltpu.SemaphoreType.DMA((phases, 8)),
            pltpu.SemaphoreType.DMA((phases, 8)),
            pltpu.SemaphoreType.DMA((ITERS,)),
            pltpu.SemaphoreType.DMA((ITERS,)),
        ],
        compiler_params=pltpu.CompilerParams(
            collective_id=0, has_side_effects=True, vmem_limit_bytes=56 * 1024 * 1024
        ),
    )(logits, target, weight, spectra, jnp.asarray(tables(extent)))
    return params, resist, losses[:ITERS, 0]


def solution(mesh):
    return jax.shard_map(
        functools.partial(on_device, mesh.shape["ty"], mesh.shape["tx"]),
        mesh=mesh,
        in_specs=(P(("slab", "ty"), "tx"), P(("slab", "ty"), "tx"), P(("slab", "ty"), "tx"), P()),
        out_specs=(P(("slab", "ty"), "tx"), P(("slab", "ty"), "tx"), P("slab")),
        check_vma=False,
    )
```

```python
import functools
import math

import jax
import jax.numpy as jnp
import numpy as np
from jax import lax
from jax.experimental import pallas as pl
from jax.experimental.pallas import tpu as pltpu
from jax.sharding import PartitionSpec as P

ITERS = 2
STEEPNESS = 4.0
THRESHOLD = 1.0
EPSILON = 1e-06
F32 = jnp.float32
BF16 = jnp.bfloat16
MESH = pl.DeviceIdType.MESH
DIRS = ((-1, 0), (1, 0), (0, -1), (0, 1), (-1, -1), (-1, 1), (1, -1), (1, 1))
OPPOSITE = tuple(DIRS.index((-dy, -dx)) for dy, dx in DIRS)


def split(x):
    high = x.astype(BF16)
    return high, (x - high.astype(F32)).astype(BF16)


def dot(a, b):
    return lax.dot_general(a, b, (((1,), (0,)), ((), ())), preferred_element_type=F32)


def dot3(left, right):
    lh, ll = left
    rh, rl = right
    return dot(jnp.concatenate([lh, ll, lh], axis=1), jnp.concatenate([rh, rh, rl], axis=0))


def sigmoid(x):
    return 1.0 / (1.0 + jnp.exp(-x))


def kernel(
    ny, nx,
    logits_ref, target_ref, weight_ref, spectra_hbm, table_ref,
    params_out, resist_out, loss_out,
    spec, t2, t3, t4, t5, t6, t7, pw, fields, total,
    send_edge, send_corner, recv_edge, recv_corner, sums_send, sums_recv,
    spec_sem, send_sem, recv_sem, sums_send_sem, sums_recv_sem,
):
    side = logits_ref.shape[0]
    extent = spec.shape[2]
    kern = spec.shape[0]
    rim = (extent - side) // 2
    ty, tx = lax.axis_index("ty"), lax.axis_index("tx")
    count = ny * nx
    me = ty * nx + tx
    pixels = float(side * side * count)

    spec_copy = pltpu.make_async_copy(spectra_hbm, spec, spec_sem)
    spec_copy.start()

    barrier = pltpu.get_barrier_semaphore()

    def peer_id(step):
        peer = lax.rem(me + step, count)
        return {"ty": peer // nx, "tx": lax.rem(peer, nx)}

    def greet(step, carry):
        pl.semaphore_signal(barrier, inc=1, device_id=peer_id(step), device_id_type=MESH)
        return carry

    lax.fori_loop(1, count, greet, 0)

    def exists(d):
        dy, dx = DIRS[d]
        ok = None
        for at, step, size in ((ty, dy, ny), (tx, dx, nx)):
            if step:
                here = at > 0 if step < 0 else at < size - 1
                ok = here if ok is None else jnp.logical_and(ok, here)
        return ok

    def buffers(d):
        return (send_edge, recv_edge, d) if d < 4 else (send_corner, recv_corner, d - 4)

    def start(phase, pieces):
        for d, piece in enumerate(pieces):
            buf, _, slot = buffers(d)
            buf[phase, slot] = piece
        for d, (dy, dx) in enumerate(DIRS):
            src, dst, slot = buffers(d)
            _, _, there = buffers(OPPOSITE[d])

            @pl.when(exists(d))
            def _():
                pltpu.make_async_remote_copy(
                    src_ref=src.at[phase, slot],
                    dst_ref=dst.at[phase, there],
                    send_sem=send_sem.at[phase, d],
                    recv_sem=recv_sem.at[phase, OPPOSITE[d]],
                    device_id={"ty": ty + dy, "tx": tx + dx},
                    device_id_type=MESH,
                ).start()

    def finish(phase):
        for d, (dy, dx) in enumerate(DIRS):
            src, dst, slot = buffers(d)

            @pl.when(exists(d))
            def _():
                pltpu.make_async_remote_copy(
                    src_ref=src.at[phase, slot],
                    dst_ref=dst.at[phase, slot],
                    send_sem=send_sem.at[phase, d],
                    recv_sem=recv_sem.at[phase, d],
                    device_id={"ty": ty + dy, "tx": tx + dx},
                    device_id_type=MESH,
                ).wait()

    def lanes(rows):
        return lax.broadcasted_iota(jnp.int32, (rows, side), 1)

    def pack(x, low):
        half = x.shape[0] // 2
        a, b = x[:half], pltpu.roll(x[half:], rim, 1)
        first = lanes(half) < rim
        return jnp.where(first, a, b) if low else jnp.where(first, b, a)

    def unpack(p):
        return jnp.concatenate([p, pltpu.roll(p, rim, 1)], axis=0)

    def rows_of(x, dy, low):
        if dy == 0:
            return x
        return x[:rim] if low else x[rim:]

    def halo_pieces(own):
        out = []
        for dy, dx in DIRS:
            piece = rows_of(own, dy, dy < 0)
            out.append(pack(piece, dx < 0) if dx else piece)
        return out

    def got(phase, dy, dx):
        _, buf, slot = buffers(DIRS.index((dy, dx)))
        value = buf[phase, slot]
        return unpack(value) if dx else value

    def halo_quads(phase, own):
        def beside(dy):
            right, left = got(phase, dy, 1), got(phase, dy, -1)
            return jnp.where(lanes(right.shape[0]) < rim, right, left)

        below = jnp.concatenate([got(phase, 1, 0), got(phase, -1, 0)], axis=0)
        corner = jnp.concatenate([beside(1), beside(-1)], axis=0)
        return ((own, beside(0)), (below, corner))

    def edge_mask(at, size, dim):
        where = lax.broadcasted_iota(jnp.int32, (side, side), dim)
        after = jnp.where(at < size - 1, rim, 0)
        before = jnp.where(at > 0, rim, side)
        return jnp.logical_or(where < after, where >= before)

    col_ok = edge_mask(tx, nx, 1)
    row_ok = edge_mask(ty, ny, 0)

    def masked(quads):
        (a, b), (c, d) = quads
        b = jnp.where(col_ok, b, 0.0)
        c = jnp.where(row_ok, c, 0.0)
        d = jnp.where(jnp.logical_and(row_ok, col_ok), d, 0.0)
        return jnp.concatenate(
            [jnp.concatenate([a, b], axis=1), jnp.concatenate([c, d], axis=1)], axis=0
        )

    def each(f, *quads):
        return tuple(tuple(f(*(q[i][j] for q in quads)) for j in range(2)) for i in range(2))

    def fold_pieces(partial):
        out = []
        for dy, dx in DIRS:
            piece = partial[side:] if dy else partial[:side]
            piece = piece[:, side:] if dx else piece[:, :side]
            piece = rows_of(piece, dy, dy > 0)
            out.append(pack(piece, dx > 0) if dx else piece)
        return out

    def fold(phase, own):
        zero = jnp.zeros((rim, side), F32)
        for d, (dy, dx) in enumerate(DIRS):
            value = got(phase, dy, dx)
            here = jnp.where(exists(d), 1, 0)
            if dx:
                lane = lanes(value.shape[0])
                near = jnp.where(lane >= rim, 1, 0) if dx > 0 else jnp.where(lane < rim, 1, 0)
                keep = near * here > 0
            else:
                keep = jnp.full(value.shape, here, jnp.int32) > 0
            value = jnp.where(keep, value, 0.0)
            if dy:
                value = jnp.concatenate([zero, value] if dy > 0 else [value, zero], axis=0)
            own = own + value
        return own

    def total_start(phase, row):
        sums_send[phase] = row
        sums_recv[phase, me] = row

        def send(step, carry):
            pltpu.make_async_remote_copy(
                src_ref=sums_send.at[phase],
                dst_ref=sums_recv.at[phase, me],
                send_sem=sums_send_sem.at[phase],
                recv_sem=sums_recv_sem.at[phase],
                device_id=peer_id(step),
                device_id_type=MESH,
            ).start()
            return carry

        lax.fori_loop(1, count, send, 0)

    def total_finish(phase):
        if count > 1:
            every = sums_recv.at[phase, pl.ds(0, count - 1)]
            pltpu.make_async_copy(every, every, sums_recv_sem.at[phase]).wait()
            pltpu.make_async_copy(every, every, sums_send_sem.at[phase]).wait()
        return jnp.sum(sums_recv[phase], axis=0)

    for part in range(2):
        cos, sin = table_ref[part, :, :extent], table_ref[part, :, extent:]
        t2[part, :extent], t2[part, extent:] = cos, sin
        cd, sd = cos[:, :side], sin[:, :side]
        unit = jnp.asarray(1.0 / (extent * extent), BF16)
        t3[part, :extent, :side], t3[part, :extent, side:] = cd * unit, sd * unit
        t3[part, extent:, :side], t3[part, extent:, side:] = -sd * unit, cd * unit
        cc, sc = cos[:side], sin[:side]
        t4[part, :side], t4[part, side:] = cc, sc
        t5[part, :side, :extent], t5[part, :side, extent:] = cc, sc
        t5[part, side:, :extent], t5[part, side:, extent:] = sc, -cc
        t6[part, :extent, :side], t6[part, :extent, side:] = cd, -sd
        t6[part, extent:, :side], t6[part, extent:, side:] = sd, cd
        t7[part, :extent, :extent], t7[part, :extent, extent:] = cos, -sin
        t7[part, extent:, :extent], t7[part, extent:, extent:] = sin, cos

    def both(ref):
        return ref[0], ref[1]

    truth = target_ref[...].astype(F32)
    weight = weight_ref[...]
    params = logits_ref[...]

    pl.semaphore_wait(barrier, count - 1)
    start(0, halo_pieces(params))
    loss_rows = []
    grad = norm = None
    for iteration in range(ITERS):
        halo_phase, fold_phase = 2 * iteration, 2 * iteration + 1
        finish(halo_phase)
        if iteration == 0:
            quads = halo_quads(halo_phase, params)
        else:
            old = each(lambda x: x, tuple(
                tuple(pw[i * side:(i + 1) * side, j * side:(j + 1) * side] for j in range(2))
                for i in range(2)))
            quads = each(lambda p, g: p - g / norm, old, halo_quads(halo_phase, grad))
        params = quads[0][0]
        if iteration + 1 < ITERS:
            for i in range(2):
                for j in range(2):
                    pw[i * side:(i + 1) * side, j * side:(j + 1) * side] = quads[i][j]
        wide = masked(each(sigmoid, quads))
        layout = wide[:side, :side]
        mixed = dot3(split(wide), both(table_ref))
        four = dot3(both(t2), split(mixed))
        trans_re = four[:extent, :extent] - four[extent:, extent:]
        trans_im = -(four[:extent, extent:] + four[extent:, :extent])
        total[0], total[1] = trans_re, trans_im
        if iteration == 0:
            spec_copy.wait()

        def forward(k, image):
            sr, si = spec[k, 0], spec[k, 1]
            tr, ti = total[0], total[1]
            prod = jnp.concatenate([tr * sr - ti * si, tr * si + ti * sr], axis=1)
            half = dot3(split(prod), both(t3))
            quad = dot3(both(t4), split(half))
            re = quad[:side, :side] - quad[side:, side:]
            im = quad[:side, side:] + quad[side:, :side]
            fields[k, :, :side] = re
            fields[k, :, side:] = im
            return image + (re * re + im * im)

        image = lax.fori_loop(0, kern, forward, jnp.zeros((side, side), F32))
        resist = sigmoid(STEEPNESS * (image - THRESHOLD))
        missed = resist - truth
        loss_rows.append(jnp.sum(weight * missed * missed, axis=0, keepdims=True))
        g_image = (2.0 * STEEPNESS) * weight * missed * resist * (1.0 - resist)
        g_image = g_image * (2.0 / (extent * extent))
        g_twice = jnp.concatenate([g_image, g_image], axis=1)
        total[...] = jnp.zeros_like(total)

        def backward(k, carry):
            back = fields[k] * g_twice
            x = dot3(split(back), both(t5))
            x = jnp.concatenate([x[:, :extent], x[:, extent:]], axis=0)
            full = dot3(both(t6), split(x))
            fr, fi = full[:extent], full[extent:]
            sr, si = spec[k, 0], spec[k, 1]
            total[0] += fr * sr - fi * si
            total[1] += fr * si + fi * sr
            return carry

        lax.fori_loop(0, kern, backward, 0)
        sums = jnp.concatenate([total[0], total[1]], axis=1)
        y = dot3(split(sums), both(t7))
        y = jnp.concatenate([y[:, :extent], y[:, extent:]], axis=0)
        partial = dot3(both(table_ref), split(y))
        start(fold_phase, fold_pieces(partial))
        finish(fold_phase)
        g_layout = fold(fold_phase, partial[:side, :side])
        grad = g_layout * layout * (1.0 - layout)
        square = jnp.sum(grad * grad, axis=0, keepdims=True)
        last = iteration + 1 == ITERS
        rows = loss_rows if last else [square] * ITERS
        total_start(iteration, jnp.concatenate([square] + rows, axis=1))
        if not last:
            start(halo_phase + 2, halo_pieces(grad))
        else:
            resist_out[...] = resist
        everyone = total_finish(iteration)
        sq_all = jnp.sum(everyone[:, :side], axis=1, keepdims=True)
        norm = jnp.sqrt(sq_all / pixels + EPSILON)
    params_out[...] = params - grad / norm
    for i in range(ITERS):
        row = everyone[:, (i + 1) * side:(i + 2) * side]
        value = jnp.sum(row, axis=1, keepdims=True) / pixels
        loss_out[i:i + 1, :] = jnp.broadcast_to(value, (1, side))


def tables(extent):
    index = np.arange(extent)
    angle = (index[:, None] * index[None, :] % extent) * (2.0 * math.pi / extent)
    exact = np.concatenate([np.cos(angle), np.sin(angle)], axis=1)
    high = exact.astype(jnp.bfloat16)
    low = (exact - high.astype(np.float64)).astype(jnp.bfloat16)
    return np.stack([high, low])


def deliver(params_ref, resist_ref, losses_ref, params_out, resist_out, losses_out):
    params_out[...] = params_ref[...]
    resist_out[...] = resist_ref[...]
    for i in range(ITERS):
        losses_out[i] = losses_ref[i, 0]


def on_device(ny, nx, logits, target, weight, spectra):
    side = logits.shape[0]
    kern, _, extent, _ = spectra.shape
    rim = (extent - side) // 2
    count = ny * nx
    phases = 2 * ITERS
    vmem = pl.BlockSpec(memory_space=pltpu.VMEM)
    params, resist, losses = pl.pallas_call(
        functools.partial(kernel, ny, nx),
        out_shape=(
            jax.ShapeDtypeStruct((side, side), F32),
            jax.ShapeDtypeStruct((side, side), F32),
            jax.ShapeDtypeStruct((8, side), F32),
        ),
        in_specs=[vmem, vmem, vmem, pl.BlockSpec(memory_space=pl.ANY), vmem],
        out_specs=(vmem, vmem, vmem),
        scratch_shapes=[
            pltpu.VMEM(spectra.shape, F32),
            pltpu.VMEM((2, 2 * extent, extent), BF16),
            pltpu.VMEM((2, 2 * extent, 2 * side), BF16),
            pltpu.VMEM((2, 2 * side, extent), BF16),
            pltpu.VMEM((2, 2 * side, 2 * extent), BF16),
            pltpu.VMEM((2, 2 * extent, 2 * side), BF16),
            pltpu.VMEM((2, 2 * extent, 2 * extent), BF16),
            pltpu.VMEM((extent, extent), F32),
            pltpu.VMEM((kern, side, 2 * side), F32),
            pltpu.VMEM((2, extent, extent), F32),
            pltpu.VMEM((phases, 4, rim, side), F32),
            pltpu.VMEM((phases, 4, rim // 2, side), F32),
            pltpu.VMEM((phases, 4, rim, side), F32),
            pltpu.VMEM((phases, 4, rim // 2, side), F32),
            pltpu.VMEM((ITERS, 1, (1 + ITERS) * side), F32),
            pltpu.VMEM((ITERS, count, 1, (1 + ITERS) * side), F32),
            pltpu.SemaphoreType.DMA,
            pltpu.SemaphoreType.DMA((phases, 8)),
            pltpu.SemaphoreType.DMA((phases, 8)),
            pltpu.SemaphoreType.DMA((ITERS,)),
            pltpu.SemaphoreType.DMA((ITERS,)),
        ],
        compiler_params=pltpu.CompilerParams(
            collective_id=0, has_side_effects=True, vmem_limit_bytes=56 * 1024 * 1024,
        ),
    )(logits, target, weight, spectra, jnp.asarray(tables(extent)))
    smem = pl.BlockSpec(memory_space=pltpu.SMEM)
    return pl.pallas_call(
        deliver,
        out_shape=(
            jax.ShapeDtypeStruct((side, side), F32),
            jax.ShapeDtypeStruct((side, side), F32),
            jax.ShapeDtypeStruct((ITERS,), F32),
        ),
        in_specs=[vmem, vmem, smem],
        out_specs=(vmem, vmem, smem),
    )(params, resist, losses)


def solution(mesh):
    return jax.shard_map(
        functools.partial(on_device, mesh.shape["ty"], mesh.shape["tx"]),
        mesh=mesh,
        in_specs=(P(("slab", "ty"), "tx"), P(("slab", "ty"), "tx"), P(("slab", "ty"), "tx"), P()),
        out_specs=(P(("slab", "ty"), "tx"), P(("slab", "ty"), "tx"), P("slab")),
        check_vma=False,
    )
```

```python
import functools
import math

import jax
import jax.numpy as jnp
import numpy as np
from jax import lax
from jax.experimental import pallas as pl
from jax.experimental.pallas import tpu as pltpu
from jax.sharding import PartitionSpec as P

ITERS = 2
STEEPNESS = 4.0
THRESHOLD = 1.0
EPSILON = 1e-06
F32 = jnp.float32
BF16 = jnp.bfloat16
MESH = pl.DeviceIdType.MESH
DIRS = ((-1, 0), (1, 0), (0, -1), (0, 1), (-1, -1), (-1, 1), (1, -1), (1, 1))
OPPOSITE = tuple(DIRS.index((-dy, -dx)) for dy, dx in DIRS)


def split(x):
    high = x.astype(BF16)
    return high, (x - high.astype(F32)).astype(BF16)


def dot(a, b):
    return lax.dot_general(a, b, (((1,), (0,)), ((), ())), preferred_element_type=F32)


def dot3(left, right):
    lh, ll = left
    rh, rl = right
    return dot(jnp.concatenate([lh, ll, lh], axis=1), jnp.concatenate([rh, rh, rl], axis=0))


def lockstep(tasks):
    steps = [None]
    while steps:
        last, steps = steps, [value for task in tasks for value in [next(task, tasks)] if value is not tasks]
    return last


def sigmoid(x):
    return 1.0 / (1.0 + jnp.exp(-x))


def kernel(
    ny, nx,
    logits_ref, target_ref, weight_ref, spectra_hbm, table_ref, turned_ref, tall_ref, flat_ref,
    params_out, resist_out, loss_out,
    spec, t2, t7, pw, fields, total,
    send_edge, send_corner, recv_edge, recv_corner, sums_send, sums_recv,
    spec_sem, send_sem, recv_sem, sums_send_sem, sums_recv_sem,
):
    side = logits_ref.shape[0]
    extent = spec.shape[2]
    kern = spec.shape[0]
    rim = (extent - side) // 2
    ty, tx = lax.axis_index("ty"), lax.axis_index("tx")
    count = ny * nx
    me = ty * nx + tx
    pixels = float(side * side * count)

    spec_copy = pltpu.make_async_copy(spectra_hbm, spec, spec_sem)
    spec_copy.start()

    barrier = pltpu.get_barrier_semaphore()

    def peer_id(step):
        peer = lax.rem(me + step, count)
        return {"ty": peer // nx, "tx": lax.rem(peer, nx)}

    def greet(step, carry):
        pl.semaphore_signal(barrier, inc=1, device_id=peer_id(step), device_id_type=MESH)
        return carry

    lax.fori_loop(1, count, greet, 0)

    def exists(d):
        dy, dx = DIRS[d]
        ok = None
        for at, step, size in ((ty, dy, ny), (tx, dx, nx)):
            if step:
                here = at > 0 if step < 0 else at < size - 1
                ok = here if ok is None else jnp.logical_and(ok, here)
        return ok

    def buffers(d):
        return (send_edge, recv_edge, d) if d < 4 else (send_corner, recv_corner, d - 4)

    def start(phase, pieces):
        for d, piece in enumerate(pieces):
            buf, _, slot = buffers(d)
            buf[phase, slot] = piece
        for d, (dy, dx) in enumerate(DIRS):
            src, dst, slot = buffers(d)
            _, _, there = buffers(OPPOSITE[d])

            @pl.when(exists(d))
            def _():
                pltpu.make_async_remote_copy(
                    src_ref=src.at[phase, slot],
                    dst_ref=dst.at[phase, there],
                    send_sem=send_sem.at[phase, d],
                    recv_sem=recv_sem.at[phase, OPPOSITE[d]],
                    device_id={"ty": ty + dy, "tx": tx + dx},
                    device_id_type=MESH,
                ).start()

    def finish(phase):
        for d, (dy, dx) in enumerate(DIRS):
            src, dst, slot = buffers(d)

            @pl.when(exists(d))
            def _():
                pltpu.make_async_remote_copy(
                    src_ref=src.at[phase, slot],
                    dst_ref=dst.at[phase, slot],
                    send_sem=send_sem.at[phase, d],
                    recv_sem=recv_sem.at[phase, d],
                    device_id={"ty": ty + dy, "tx": tx + dx},
                    device_id_type=MESH,
                ).wait()

    def lanes(rows):
        return lax.broadcasted_iota(jnp.int32, (rows, side), 1)

    def pack(x, low):
        half = x.shape[0] // 2
        a, b = x[:half], pltpu.roll(x[half:], rim, 1)
        first = lanes(half) < rim
        return jnp.where(first, a, b) if low else jnp.where(first, b, a)

    def unpack(p):
        return jnp.concatenate([p, pltpu.roll(p, rim, 1)], axis=0)

    def rows_of(x, dy, low):
        if dy == 0:
            return x
        return x[:rim] if low else x[rim:]

    def halo_pieces(own):
        out = []
        for dy, dx in DIRS:
            piece = rows_of(own, dy, dy < 0)
            out.append(pack(piece, dx < 0) if dx else piece)
        return out

    def got(phase, dy, dx):
        _, buf, slot = buffers(DIRS.index((dy, dx)))
        value = buf[phase, slot]
        return unpack(value) if dx else value

    def halo_quads(phase, own):
        def beside(dy):
            right, left = got(phase, dy, 1), got(phase, dy, -1)
            return jnp.where(lanes(right.shape[0]) < rim, right, left)

        below = jnp.concatenate([got(phase, 1, 0), got(phase, -1, 0)], axis=0)
        corner = jnp.concatenate([beside(1), beside(-1)], axis=0)
        return ((own, beside(0)), (below, corner))

    def edge_mask(at, size, dim):
        where = lax.broadcasted_iota(jnp.int32, (side, side), dim)
        after = jnp.where(at < size - 1, rim, 0)
        before = jnp.where(at > 0, rim, side)
        return jnp.logical_or(where < after, where >= before)

    col_ok = edge_mask(tx, nx, 1)
    row_ok = edge_mask(ty, ny, 0)

    def masked(quads):
        (a, b), (c, d) = quads
        b = jnp.where(col_ok, b, 0.0)
        c = jnp.where(row_ok, c, 0.0)
        d = jnp.where(jnp.logical_and(row_ok, col_ok), d, 0.0)
        return jnp.concatenate(
            [jnp.concatenate([a, b], axis=1), jnp.concatenate([c, d], axis=1)], axis=0
        )

    def each(f, *quads):
        return tuple(tuple(f(*(q[i][j] for q in quads)) for j in range(2)) for i in range(2))

    def fold_pieces(partial):
        out = []
        for dy, dx in DIRS:
            piece = partial[side:] if dy else partial[:side]
            piece = piece[:, side:] if dx else piece[:, :side]
            piece = rows_of(piece, dy, dy > 0)
            out.append(pack(piece, dx > 0) if dx else piece)
        return out

    def fold(phase, own):
        zero = jnp.zeros((rim, side), F32)
        for d, (dy, dx) in enumerate(DIRS):
            value = got(phase, dy, dx)
            here = jnp.where(exists(d), 1, 0)
            if dx:
                lane = lanes(value.shape[0])
                near = jnp.where(lane >= rim, 1, 0) if dx > 0 else jnp.where(lane < rim, 1, 0)
                keep = near * here > 0
            else:
                keep = jnp.full(value.shape, here, jnp.int32) > 0
            value = jnp.where(keep, value, 0.0)
            if dy:
                value = jnp.concatenate([zero, value] if dy > 0 else [value, zero], axis=0)
            own = own + value
        return own

    def total_start(phase, row):
        sums_send[phase] = row
        sums_recv[phase, me] = row

        def send(step, carry):
            pltpu.make_async_remote_copy(
                src_ref=sums_send.at[phase],
                dst_ref=sums_recv.at[phase, me],
                send_sem=sums_send_sem.at[phase],
                recv_sem=sums_recv_sem.at[phase],
                device_id=peer_id(step),
                device_id_type=MESH,
            ).start()
            return carry

        lax.fori_loop(1, count, send, 0)

    def total_finish(phase):
        if count > 1:
            every = sums_recv.at[phase, pl.ds(0, count - 1)]
            pltpu.make_async_copy(every, every, sums_recv_sem.at[phase]).wait()
            pltpu.make_async_copy(every, every, sums_send_sem.at[phase]).wait()
        return jnp.sum(sums_recv[phase], axis=0)

    for part in range(2):
        cos, sin = turned_ref[part, :, :extent], turned_ref[part, :, extent:]
        t2[part, :extent], t2[part, extent:] = cos, sin
        t7[part, :extent, :extent], t7[part, :extent, extent:] = cos, -sin
        t7[part, extent:, :extent], t7[part, extent:, extent:] = sin, cos

    def both(ref):
        return ref[0], ref[1]

    mid = side // 2
    first = lanes(side) < mid

    def shuffle(transposed):
        at = lax.broadcasted_iota(jnp.int32, (side, side), 1 if transposed else 0)
        of = lax.broadcasted_iota(jnp.int32, (side, side), 0 if transposed else 1)
        return jnp.where(of == jnp.where(at < mid, at + mid, side - 1 - at), 1.0, 0.0).astype(BF16)

    def moved(x, left, right):
        out = jnp.zeros_like(x)
        for _ in range(3):
            piece = x.astype(BF16)
            x = x - piece.astype(F32)
            out = out + dot(dot(left, piece).astype(BF16), right)
        return out

    there, back_again = shuffle(False), shuffle(True)
    truth = moved(target_ref[...].astype(F32), there, back_again)
    weight = moved(weight_ref[...], there, back_again)

    def turn(x):
        return pltpu.roll(x, mid, 1)

    def signed(x):
        rolled = turn(x)
        return jnp.where(first, x, rolled), jnp.where(first, rolled, -x)
    params = logits_ref[...]

    pl.semaphore_wait(barrier, count - 1)
    start(0, halo_pieces(params))
    loss_rows = []
    grad = norm = None
    for iteration in range(ITERS):
        halo_phase, fold_phase = 2 * iteration, 2 * iteration + 1
        finish(halo_phase)
        if iteration == 0:
            quads = halo_quads(halo_phase, params)
        else:
            old = each(lambda x: x, tuple(
                tuple(pw[i * side:(i + 1) * side, j * side:(j + 1) * side] for j in range(2))
                for i in range(2)))
            quads = each(lambda p, g: p - g / norm, old, halo_quads(halo_phase, grad))
        params = quads[0][0]
        if iteration + 1 < ITERS:
            for i in range(2):
                for j in range(2):
                    pw[i * side:(i + 1) * side, j * side:(j + 1) * side] = quads[i][j]
        wide = masked(each(sigmoid, quads))
        layout = wide[:side, :side]
        mixed = dot3(split(wide), both(table_ref))
        four = dot3(both(t2), split(mixed))
        trans_re = four[:extent, :extent] - four[extent:, extent:]
        trans_im = -(four[:extent, extent:] + four[extent:, :extent])
        unit = 1.0 / (extent * extent)
        total[0], total[1] = trans_re * unit, trans_im * unit
        if iteration == 0:
            spec_copy.wait()

        def forward(k):
            sr, si = spec[k, 0], spec[k, 1]
            tr, ti = total[0], total[1]
            prod = jnp.concatenate([tr * sr - ti * si, tr * si + ti * sr], axis=0)
            ph, pl_low = split(prod)
            yield
            th, tl = tall_ref[0], tall_ref[1]
            wide_half = dot(ph, jnp.concatenate([th, tl], axis=1))
            half = wide_half[:, :side] + (wide_half[:, side:] + dot(pl_low, th))
            half = jnp.concatenate([half[:extent], half[extent:]], axis=1)
            yield
            quad = dot3(both(flat_ref), split(half))
            yield
            rc, rs = signed(quad[:, :side])
            ic, js = signed(quad[:, side:])
            even, odd = rc[:mid] - js[:mid], rs[mid:] + ic[mid:]
            re = jnp.concatenate([even - odd, even + odd], axis=0)
            even, odd = ic[:mid] + rs[:mid], rc[mid:] - js[mid:]
            im = jnp.concatenate([even + odd, even - odd], axis=0)
            fields[k, :, :side] = re
            fields[k, :, side:] = im
            yield re * re + im * im

        def imaged(ks, image):
            for part in lockstep([forward(k) for k in ks]):
                image = image + part
            return image

        image = lax.fori_loop(
            0, kern // 2, lambda i, image: imaged((2 * i, 2 * i + 1), image), jnp.zeros((side, side), F32)
        )
        if kern % 2:
            image = imaged((kern - 1,), image)
        resist = sigmoid(STEEPNESS * (image - THRESHOLD))
        missed = resist - truth
        loss_rows.append(jnp.sum(weight * missed * missed, axis=0, keepdims=True))
        g_image = (2.0 * STEEPNESS) * weight * missed * resist * (1.0 - resist)
        g_image = g_image * (2.0 / (extent * extent))
        g_twice = jnp.concatenate([g_image, g_image], axis=1)
        total[...] = jnp.zeros_like(total)

        def backward(k):
            back = fields[k] * g_twice
            br, bi = back[:, :side], back[:, side:]
            tr, ti = turn(br), turn(bi)
            z = jnp.concatenate(
                [jnp.where(first, br + tr, ti - bi), jnp.where(first, -(bi + ti), tr - br)], axis=0
            )
            zh, zl = split(z)
            yield
            fh, fl = flat_ref[0], flat_ref[1]
            x = dot(jnp.concatenate([zh, zl], axis=1), jnp.concatenate([fh, fh], axis=0)) + dot(zh, fl)
            rp, rm, ip, im = (x[n * mid:(n + 1) * mid] for n in range(4))
            u = jnp.concatenate(
                [jnp.concatenate([rp + rm, im - ip], axis=0),
                 jnp.concatenate([ip + im, rp - rm], axis=0)], axis=1
            )
            uh, ul = split(u)
            yield
            th, tl = tall_ref[0], tall_ref[1]
            full = dot(jnp.concatenate([th, th], axis=1), jnp.concatenate([uh, ul], axis=0)) + dot(tl, uh)
            yield
            fr, fi = full[:, :extent], full[:, extent:]
            sr, si = spec[k, 0], spec[k, 1]
            yield fr * sr - fi * si, fr * si + fi * sr

        def gathered(ks, carry):
            parts = lockstep([backward(k) for k in ks])
            total[0] += sum(part[0] for part in parts)
            total[1] += sum(part[1] for part in parts)
            return carry

        lax.fori_loop(0, kern // 2, lambda i, carry: gathered((2 * i, 2 * i + 1), carry), 0)
        if kern % 2:
            gathered((kern - 1,), 0)
        sums = jnp.concatenate([total[0], total[1]], axis=1)
        y = dot3(split(sums), both(t7))
        y = jnp.concatenate([y[:, :extent], y[:, extent:]], axis=0)
        partial = dot3(both(table_ref), split(y))
        start(fold_phase, fold_pieces(partial))
        finish(fold_phase)
        g_layout = fold(fold_phase, partial[:side, :side])
        grad = g_layout * layout * (1.0 - layout)
        square = jnp.sum(grad * grad, axis=0, keepdims=True)
        last = iteration + 1 == ITERS
        rows = loss_rows if last else [square] * ITERS
        total_start(iteration, jnp.concatenate([square] + rows, axis=1))
        if not last:
            start(halo_phase + 2, halo_pieces(grad))
        else:
            resist_out[...] = moved(resist, back_again, there)
        everyone = total_finish(iteration)
        sq_all = jnp.sum(everyone[:, :side], axis=1, keepdims=True)
        norm = jnp.sqrt(sq_all / pixels + EPSILON)
    params_out[...] = params - grad / norm
    for i in range(ITERS):
        row = everyone[:, (i + 1) * side:(i + 2) * side]
        value = jnp.sum(row, axis=1, keepdims=True) / pixels
        loss_out[i:i + 1, :] = jnp.broadcast_to(value, (1, side))


def two_parts(exact):
    high = exact.astype(jnp.bfloat16)
    return jnp.asarray(np.stack([high, (exact - high.astype(np.float64)).astype(jnp.bfloat16)]))


def tables(extent, side):
    rim = (extent - side) // 2
    index = np.arange(extent)
    pixel = np.where(index < extent - rim, index, index - extent) - side / 2 + 0.5
    near = np.arange(side // 2) + 0.5
    step = 2.0 * math.pi / extent
    angle = pixel[:, None] * index[None, :] * step
    close = near[:, None] * index[None, :] * step
    flat = np.concatenate([np.cos(close), np.sin(close)], axis=0)
    return (
        two_parts(np.concatenate([np.cos(angle), np.sin(angle)], axis=1)),
        two_parts(np.concatenate([np.cos(angle).T, np.sin(angle).T], axis=1)),
        two_parts(flat.T),
        two_parts(flat),
    )


def deliver(params_ref, resist_ref, losses_ref, params_out, resist_out, losses_out):
    params_out[...] = params_ref[...]
    resist_out[...] = resist_ref[...]
    for i in range(ITERS):
        losses_out[i] = losses_ref[i, 0]


def on_device(ny, nx, logits, target, weight, spectra):
    side = logits.shape[0]
    kern, _, extent, _ = spectra.shape
    rim = (extent - side) // 2
    count = ny * nx
    phases = 2 * ITERS
    vmem = pl.BlockSpec(memory_space=pltpu.VMEM)
    params, resist, losses = pl.pallas_call(
        functools.partial(kernel, ny, nx),
        out_shape=(
            jax.ShapeDtypeStruct((side, side), F32),
            jax.ShapeDtypeStruct((side, side), F32),
            jax.ShapeDtypeStruct((8, side), F32),
        ),
        in_specs=[vmem, vmem, vmem, pl.BlockSpec(memory_space=pl.ANY)] + [vmem] * 4,
        out_specs=(vmem, vmem, vmem),
        scratch_shapes=[
            pltpu.VMEM(spectra.shape, F32),
            pltpu.VMEM((2, 2 * extent, extent), BF16),
            pltpu.VMEM((2, 2 * extent, 2 * extent), BF16),
            pltpu.VMEM((extent, extent), F32),
            pltpu.VMEM((kern, side, 2 * side), F32),
            pltpu.VMEM((2, extent, extent), F32),
            pltpu.VMEM((phases, 4, rim, side), F32),
            pltpu.VMEM((phases, 4, rim // 2, side), F32),
            pltpu.VMEM((phases, 4, rim, side), F32),
            pltpu.VMEM((phases, 4, rim // 2, side), F32),
            pltpu.VMEM((ITERS, 1, (1 + ITERS) * side), F32),
            pltpu.VMEM((ITERS, count, 1, (1 + ITERS) * side), F32),
            pltpu.SemaphoreType.DMA,
            pltpu.SemaphoreType.DMA((phases, 8)),
            pltpu.SemaphoreType.DMA((phases, 8)),
            pltpu.SemaphoreType.DMA((ITERS,)),
            pltpu.SemaphoreType.DMA((ITERS,)),
        ],
        compiler_params=pltpu.CompilerParams(
            collective_id=0, has_side_effects=True, vmem_limit_bytes=56 * 1024 * 1024,
        ),
    )(logits, target, weight, spectra, *tables(extent, side))
    smem = pl.BlockSpec(memory_space=pltpu.SMEM)
    return pl.pallas_call(
        deliver,
        out_shape=(
            jax.ShapeDtypeStruct((side, side), F32),
            jax.ShapeDtypeStruct((side, side), F32),
            jax.ShapeDtypeStruct((ITERS,), F32),
        ),
        in_specs=[vmem, vmem, smem],
        out_specs=(vmem, vmem, smem),
    )(params, resist, losses)


def solution(mesh):
    return jax.shard_map(
        functools.partial(on_device, mesh.shape["ty"], mesh.shape["tx"]),
        mesh=mesh,
        in_specs=(P(("slab", "ty"), "tx"), P(("slab", "ty"), "tx"), P(("slab", "ty"), "tx"), P()),
        out_specs=(P(("slab", "ty"), "tx"), P(("slab", "ty"), "tx"), P("slab")),
        check_vma=False,
    )
```
